32 devices in a mesh: seq: 8 (over z, y), head: 4 (over x, core).
Axes of the slice: x: 2, y: 2, z: 4, core: 2. Of those that a mesh axis runs over, the one named last changes fastest.
Arguments:
- hidden_in: bfloat16 [4096, 1024], P('seq', 'head'), may hold values from -6 to 6
- norm_gain: float32 [1024], replicated, may hold values from 0.5 to 1.5
- proj_gate: bfloat16 [1024, 2048], P(None, 'head'), may hold values from -0.1875 to 0.1875
- proj_value: bfloat16 [1024, 2048], P(None, 'head'), may hold values from -0.1875 to 0.1875
- proj_inout: bfloat16 [1024, 256], replicated, may hold values from -0.1875 to 0.1875
- proj_step: bfloat16 [1024, 32], P(None, 'head'), may hold values from -0.1875 to 0.1875
- conv_value: float32 [4, 2048], P(None, 'head'), may hold values from -3 to 3
- conv_bias_value: float32 [2048], P('head'), may hold values from -3 to 3
- conv_inout: float32 [4, 256], replicated, may hold values from -3 to 3
- conv_bias_inout: float32 [256], replicated, may hold values from -3 to 3
- step_bias: float32 [32], P('head'), may hold values from -5 to -1
- decay_log: float32 [32], P('head'), may hold values from -9 to 0
- skip_gain: float32 [32], P('head'), may hold values from 0.5 to 1.5
- gate_gain: float32 [2048], P('head'), may hold values from 0.5 to 1.5
- proj_out: bfloat16 [2048, 1024], P('head'), may hold values from -0.125 to 0.125
- out_grad: bfloat16 [4096, 1024], P('seq', 'head'), may hold values from -6 to 6
- doc_starts: int32 [4], replicated, may hold values from 0 to 4095, as said below
Outputs:
- block_out: bfloat16 [4096, 1024], P('seq', 'head')
- grad_in: float32 [4096, 1024], P('seq', 'head')
- grad_norm_gain: float32 [1024], P('head')
- grad_proj_gate: float32 [1024, 2048], P('seq', 'head')
- grad_proj_value: float32 [1024, 2048], P('seq', 'head')
- grad_proj_inout: float32 [1024, 256], P('seq', 'head')
- grad_proj_step: float32 [1024, 32], P('seq', 'head')
- grad_conv_value: float32 [4, 2048], P(None, 'head')
- grad_conv_bias_value: float32 [2048], P('head')
- grad_conv_inout: float32 [4, 256], P(None, 'head')
- grad_conv_bias_inout: float32 [256], P('head')
- grad_step_bias: float32 [32], P('head')
- grad_decay_log: float32 [32], P('head')
- grad_skip_gain: float32 [32], P('head')
- grad_gate_gain: float32 [2048], P('head')
- grad_proj_out: float32 [2048, 1024], P('head', 'seq')
The draws below stay inside these ranges and needn't reach their ends.
Inputs may be any that keep to these rules, and one draw needn't show every extreme that they name: `doc_starts`: the first entry is 0 and the entries rise strictly; each is the first position of a document in the packed row of 4096 tokens; the last document is the single token at position 4095.
All inputs are finite; a program needn't handle non-finite values.
Results may differ from the reference program's by a relative error of at most 0.002.
The reference program's roundings to bfloat16 on the way count: a program that leaves them out, or rounds other values in their place, can miss the bound.
Values may be sent and summed in bfloat16 or wider, within the bound.
A program may use at most 128 MiB of HBM per device.

```python
import jax
import jax.numpy as jnp
from jax import lax

D = 1024
H = 32
P_SIZE = 64
N = 128
CONV = 4
BLOCK = 256
NDOC = 4
DI = 2048
TOKENS = 4096


def draw_decay_log(key, part):
    return jax.random.uniform(key, (H,), jnp.float32, -9.0, 0.0)


def draw_doc_starts(key, part):
    picks = jax.random.choice(key, TOKENS - 2, (NDOC - 2,), replace=False) + 1
    picks = jnp.sort(picks.astype(jnp.int32))
    last = jnp.full((1,), TOKENS - 1, jnp.int32)
    return jnp.concatenate([jnp.zeros((1,), jnp.int32), picks, last])


def shard_levels(key, shape, shards, low, largest):
    def one(dim, blocks):
        steps = jax.random.uniform(jax.random.fold_in(jax.random.fold_in(key, 6), dim), (blocks,), jnp.float32, low / len(shards), largest / len(shards))
        return jnp.repeat(jnp.exp(steps), shape[dim] // blocks).reshape((-1,) + (1,) * (len(shape) - dim - 1))

    factor_of = one(*shards[0])
    for cut in shards[1:]:
        factor_of = factor_of * one(*cut)
    return factor_of


def gaussian(key, extent, scale, bound, shards=(), kind=jnp.bfloat16):
    values = scale * jax.random.normal(key, extent, jnp.float32)
    if shards:
        values = values * shard_levels(key, extent, shards, -0.22, 0.18)
    return jnp.clip(values, -bound, bound).astype(kind)


def setup_inputs(seed: int = 0) -> dict:
    seeds = jax.random.split(jax.random.key(seed), 18)
    hidden_in = gaussian(seeds[0], (TOKENS, D), 1.0, 6.0, ((0, 8), (1, 4)))
    norm_gain = jnp.clip(1.0 + 0.1 * jax.random.normal(seeds[1], (D,), jnp.float32), 0.5, 1.5)
    proj_gate = gaussian(seeds[2], (D, DI), D ** -0.5, 0.1875, ((1, 4),))
    proj_value = gaussian(seeds[3], (D, DI), D ** -0.5, 0.1875, ((1, 4),))
    proj_inout = gaussian(seeds[4], (D, 2 * N), D ** -0.5, 0.1875)
    proj_step = gaussian(seeds[5], (D, H), D ** -0.5, 0.1875, ((1, 4),))
    conv_value = gaussian(seeds[6], (CONV, DI), CONV ** -0.5, 3.0, ((1, 4),), jnp.float32)
    conv_bias_value = gaussian(seeds[7], (DI,), 0.5, 3.0, ((0, 4),), jnp.float32)
    conv_inout = gaussian(seeds[8], (CONV, 2 * N), CONV ** -0.5, 3.0, (), jnp.float32)
    conv_bias_inout = gaussian(seeds[9], (2 * N,), 0.5, 3.0, (), jnp.float32)
    step_bias = jnp.clip(-5.0 + 4.0 * jax.random.uniform(seeds[10], (H,), jnp.float32) ** shard_levels(seeds[10], (H,), ((0, 4),), -0.2, 0.2), -5.0, -1.0)
    decay_log = draw_decay_log(jax.random.fold_in(seeds[17], 71), 0)
    skip_gain = jnp.clip(0.5 + 1.0 * jax.random.uniform(seeds[12], (H,), jnp.float32) ** shard_levels(seeds[12], (H,), ((0, 4),), -0.2, 0.2), 0.5, 1.5)
    gate_gain = jnp.clip(1.0 + 0.1 * jax.random.normal(seeds[13], (DI,), jnp.float32), 0.5, 1.5)
    proj_out = gaussian(seeds[14], (DI, D), DI ** -0.5, 0.125, ((0, 4),))
    out_grad = gaussian(seeds[15], (TOKENS, D), 1.0, 6.0, ((0, 8), (1, 4)))
    doc_starts = draw_doc_starts(jax.random.fold_in(seeds[17], 71), 0)
    return {"hidden_in": hidden_in, "norm_gain": norm_gain, "proj_gate": proj_gate, "proj_value": proj_value, "proj_inout": proj_inout, "proj_step": proj_step, "conv_value": conv_value, "conv_bias_value": conv_bias_value, "conv_inout": conv_inout, "conv_bias_inout": conv_bias_inout, "step_bias": step_bias, "decay_log": decay_log, "skip_gain": skip_gain, "gate_gain": gate_gain, "proj_out": proj_out, "out_grad": out_grad, "doc_starts": doc_starts}


EPSILON = 1e-05
PRECISE = lax.Precision.HIGHEST

def plain_dot(left, right):
    return jnp.dot(left, right, preferred_element_type=jnp.float32)

def silu_slope(value):
    sigma = jax.nn.sigmoid(value)
    return sigma * (1.0 + value * (1.0 - sigma))

def doc_number(doc_starts, positions):
    return lax.optimization_barrier(jnp.sum((doc_starts[None, :] <= positions[:, None]).astype(jnp.int32), axis=1))

def block_terms(log_decay, doc_block, doc_before):
    cum_decay = jnp.cumsum(log_decay, axis=0)
    causal = jnp.arange(BLOCK)[:, None] >= jnp.arange(BLOCK)[None, :]
    same = (doc_block[:, None] == doc_block[None, :]) & causal
    spread = cum_decay.T[:, :, None] - cum_decay.T[:, None, :]
    decay = jnp.where(same[None], jnp.exp(jnp.minimum(spread, 0.0)), 0.0)
    carry_in = jnp.where((doc_block == doc_before)[:, None], jnp.exp(cum_decay), 0.0)
    to_end = jnp.where((doc_block == doc_block[-1])[:, None], jnp.exp(cum_decay[-1][None, :] - cum_decay), 0.0)
    whole = jnp.where(doc_block[-1] == doc_before, jnp.exp(cum_decay[-1]), 0.0)
    return (decay, carry_in, to_end, whole)

def block_forward_local(scaled, in_mat, out_mat, log_decay, doc_block, doc_before):
    decay, carry_in, to_end, whole = block_terms(log_decay, doc_block, doc_before)
    scores = jnp.dot(out_mat, in_mat.T, precision=PRECISE)
    y_inner = jnp.einsum('hij,ij,jhp->ihp', decay, scores, scaled, precision=PRECISE)
    block_state = jnp.einsum('jh,jhp,jn->hpn', to_end, scaled, in_mat, precision=PRECISE)
    return (y_inner, block_state, whole, carry_in)

def block_local_grad(grad_y, scaled, in_mat, out_mat, log_decay, doc_block, doc_before, state):
    decay, carry_in, to_end, whole = block_terms(log_decay, doc_block, doc_before)
    scores = jnp.dot(out_mat, in_mat.T, precision=PRECISE)
    inner = jnp.einsum('ihp,jhp->hij', grad_y, scaled, precision=PRECISE)
    grad_scores = lax.optimization_barrier(jnp.sum(inner * decay, axis=0))
    grad_decay = inner * scores[None] * decay
    grad_cum = lax.optimization_barrier(jnp.sum(grad_decay, axis=2)).T - lax.optimization_barrier(jnp.sum(grad_decay, axis=1)).T
    grad_scaled = jnp.einsum('hij,ij,ihp->jhp', decay, scores, grad_y, precision=PRECISE)
    grad_out = jnp.dot(grad_scores, in_mat, precision=PRECISE)
    grad_in = jnp.dot(grad_scores.T, out_mat, precision=PRECISE)
    readout = jnp.einsum('in,hpn->ihp', out_mat, state, precision=PRECISE)
    grad_cum = grad_cum + lax.optimization_barrier(jnp.sum(grad_y * readout, axis=2)) * carry_in
    grad_out = grad_out + jnp.einsum('ih,ihp,hpn->in', carry_in, grad_y, state, precision=PRECISE)
    local_grad = jnp.einsum('ih,ihp,in->hpn', carry_in, grad_y, out_mat, precision=PRECISE)
    return (grad_scaled, grad_in, grad_out, grad_cum, local_grad, to_end, whole)

def block_state_grad(grad_after, scaled, in_mat, to_end, whole, state, grad_cum):
    grad_end = jnp.einsum('hpn,jhp,jn->jh', grad_after, scaled, in_mat, precision=PRECISE)
    more_scaled = jnp.einsum('jh,jn,hpn->jhp', to_end, in_mat, grad_after, precision=PRECISE)
    more_in = jnp.einsum('jh,jhp,hpn->jn', to_end, scaled, grad_after, precision=PRECISE)
    weighted = grad_end * to_end
    grad_whole = lax.optimization_barrier(jnp.sum(grad_after * state, axis=(1, 2)))
    grad_cum = grad_cum - weighted
    grad_cum = grad_cum.at[-1].add(lax.optimization_barrier(jnp.sum(weighted, axis=0)) + grad_whole * whole)
    grad_log = jnp.cumsum(grad_cum[::-1], axis=0)[::-1]
    return (more_scaled, more_in, grad_log)

def forward_block(state, inputs):
    scaled, in_mat, out_mat, log_decay, doc_block, doc_before = inputs
    y_inner, block_state, whole, carry_in = block_forward_local(scaled, in_mat, out_mat, log_decay, doc_block, doc_before)
    y_state = carry_in[:, :, None] * jnp.einsum('in,hpn->ihp', out_mat, state, precision=PRECISE)
    return (whole[:, None, None] * state + block_state, (y_inner + y_state, state))

def backward_block(grad_after, inputs):
    grad_y, scaled, in_mat, out_mat, log_decay, doc_block, doc_before, state = inputs
    grad_scaled, grad_in, grad_out, grad_cum, local_grad, to_end, whole = block_local_grad(grad_y, scaled, in_mat, out_mat, log_decay, doc_block, doc_before, state)
    more_scaled, more_in, grad_log = block_state_grad(grad_after, scaled, in_mat, to_end, whole, state, grad_cum)
    grad_before = whole[:, None, None] * grad_after + local_grad
    return (grad_before, (grad_scaled + more_scaled, grad_in + more_in, grad_out, grad_log))

def reference(hidden_in, norm_gain, proj_gate, proj_value, proj_inout, proj_step, conv_value, conv_bias_value, conv_inout, conv_bias_inout, step_bias, decay_log, skip_gain, gate_gain, proj_out, out_grad, doc_starts):
    num_blocks = TOKENS // BLOCK
    margin = CONV - 1
    doc_ids = doc_number(doc_starts, jnp.arange(TOKENS, dtype=jnp.int32))
    doc_before = doc_number(doc_starts, jnp.arange(num_blocks, dtype=jnp.int32) * BLOCK - 1)
    doc_margin = doc_number(doc_starts, jnp.arange(margin, dtype=jnp.int32) - margin)
    x_float = hidden_in.astype(jnp.float32)
    inv_rms = lax.rsqrt(lax.optimization_barrier(jnp.mean(x_float * x_float, axis=1)) + EPSILON)
    normed = (x_float * inv_rms[:, None] * norm_gain[None, :]).astype(jnp.bfloat16)
    gate_pre = plain_dot(normed, proj_gate)
    conv_in = jnp.concatenate([plain_dot(normed, proj_value), plain_dot(normed, proj_inout)], axis=1).astype(jnp.bfloat16)
    step_raw = plain_dot(normed, proj_step)
    conv_pad = jnp.concatenate([jnp.zeros((margin, DI + 2 * N), jnp.float32), conv_in.astype(jnp.float32)], axis=0)
    doc_pad = jnp.concatenate([doc_margin, doc_ids])
    conv_weight = jnp.concatenate([conv_value, conv_inout], axis=1)
    conv_bias = jnp.concatenate([conv_bias_value, conv_bias_inout])
    lag_masks = [(doc_pad[margin - offset:margin - offset + TOKENS] == doc_ids).astype(jnp.float32)[:, None] for offset in range(CONV)]
    lagged = [conv_pad[margin - offset:margin - offset + TOKENS] for offset in range(CONV)]
    conv_pre = conv_bias[None, :] + sum((conv_weight[offset][None, :] * lagged[offset] * lag_masks[offset] for offset in range(CONV)))
    conv_act = jax.nn.silu(conv_pre)
    values = conv_act[:, :DI].reshape(TOKENS, H, P_SIZE)
    in_mat = conv_act[:, DI:DI + N]
    out_mat = conv_act[:, DI + N:]
    step_size = jax.nn.softplus(step_raw + step_bias[None, :])
    decay_rate = -jnp.exp(decay_log)
    log_decay = step_size * decay_rate[None, :]
    scaled = values * step_size[:, :, None]

    def by_block(array):
        return array.reshape((num_blocks, BLOCK) + array.shape[1:])
    blocked = (by_block(scaled), by_block(in_mat), by_block(out_mat), by_block(log_decay), by_block(doc_ids), doc_before)
    _, (y_blocks, states) = lax.scan(forward_block, jnp.zeros((H, P_SIZE, N), jnp.float32), blocked)
    y_ssd = y_blocks.reshape(TOKENS, H, P_SIZE) + skip_gain[None, :, None] * values
    y_flat = y_ssd.reshape(TOKENS, DI)
    gate_act = jax.nn.silu(gate_pre)
    gated = y_flat * gate_act
    inv_gate = lax.rsqrt(lax.optimization_barrier(jnp.mean(gated * gated, axis=1)) + EPSILON)
    normed_gate = (gated * inv_gate[:, None] * gate_gain[None, :]).astype(jnp.bfloat16)
    block_out = (x_float + plain_dot(normed_gate, proj_out)).astype(jnp.bfloat16)
    grad_proj_out = plain_dot(normed_gate.T, out_grad)
    grad_normed_gate = plain_dot(out_grad, proj_out.T)
    grad_gate_gain = lax.optimization_barrier(jnp.sum(grad_normed_gate * gated * inv_gate[:, None], axis=0))
    gate_term = grad_normed_gate * gate_gain[None, :]
    grad_gated = inv_gate[:, None] * gate_term - gated * (inv_gate ** 3 * lax.optimization_barrier(jnp.mean(gate_term * gated, axis=1)))[:, None]
    grad_y = (grad_gated * gate_act).reshape(TOKENS, H, P_SIZE)
    grad_gate_pre = grad_gated * y_flat * silu_slope(gate_pre)
    grad_skip_gain = lax.optimization_barrier(jnp.sum(grad_y * values, axis=(0, 2)))
    back_inputs = (by_block(grad_y),) + blocked + (states,)
    _, (grad_scaled, grad_in_mat, grad_out_mat, grad_log) = lax.scan(backward_block, jnp.zeros((H, P_SIZE, N), jnp.float32), back_inputs, reverse=True)
    grad_scaled = grad_scaled.reshape(TOKENS, H, P_SIZE)
    grad_in_mat = grad_in_mat.reshape(TOKENS, N)
    grad_out_mat = grad_out_mat.reshape(TOKENS, N)
    grad_log = grad_log.reshape(TOKENS, H)
    grad_values = grad_scaled * step_size[:, :, None] + skip_gain[None, :, None] * grad_y
    grad_step = grad_log * decay_rate[None, :] + lax.optimization_barrier(jnp.sum(grad_scaled * values, axis=2))
    grad_decay_log = lax.optimization_barrier(jnp.sum(grad_log * step_size, axis=0)) * decay_rate
    grad_step_raw = grad_step * jax.nn.sigmoid(step_raw + step_bias[None, :])
    grad_step_bias = lax.optimization_barrier(jnp.sum(grad_step_raw, axis=0))
    grad_act = jnp.concatenate([grad_values.reshape(TOKENS, DI), grad_in_mat, grad_out_mat], axis=1)
    grad_conv_pre = grad_act * silu_slope(conv_pre)
    grad_conv = jnp.stack([lax.optimization_barrier(jnp.sum(grad_conv_pre * lagged[offset] * lag_masks[offset], axis=0)) for offset in range(CONV)])
    grad_conv_bias = lax.optimization_barrier(jnp.sum(grad_conv_pre, axis=0))
    grad_conv_in = sum((jnp.concatenate([(grad_conv_pre * conv_weight[offset][None, :] * lag_masks[offset])[offset:], jnp.zeros((offset, DI + 2 * N), jnp.float32)], axis=0) for offset in range(CONV)))
    grad_gate_b = grad_gate_pre.astype(jnp.bfloat16)
    grad_value_b = grad_conv_in[:, :DI].astype(jnp.bfloat16)
    grad_inout_b = grad_conv_in[:, DI:].astype(jnp.bfloat16)
    grad_step_b = grad_step_raw.astype(jnp.bfloat16)
    grad_proj_gate = plain_dot(normed.T, grad_gate_b)
    grad_proj_value = plain_dot(normed.T, grad_value_b)
    grad_proj_inout = plain_dot(normed.T, grad_inout_b)
    grad_proj_step = plain_dot(normed.T, grad_step_b)
    grad_normed = plain_dot(grad_gate_b, proj_gate.T) + plain_dot(grad_value_b, proj_value.T) + plain_dot(grad_inout_b, proj_inout.T) + plain_dot(grad_step_b, proj_step.T)
    grad_norm_gain = lax.optimization_barrier(jnp.sum(grad_normed * x_float * inv_rms[:, None], axis=0))
    norm_term = grad_normed * norm_gain[None, :]
    grad_in = out_grad.astype(jnp.float32) + inv_rms[:, None] * norm_term - x_float * (inv_rms ** 3 * lax.optimization_barrier(jnp.mean(norm_term * x_float, axis=1)))[:, None]
    return (block_out, grad_in, grad_norm_gain, grad_proj_gate, grad_proj_value, grad_proj_inout, grad_proj_step, grad_conv[:, :DI], grad_conv_bias[:DI], grad_conv[:, DI:], grad_conv_bias[DI:], grad_step_bias, grad_decay_log, grad_skip_gain, grad_gate_gain, grad_proj_out)
```

```python
import jax
import jax.numpy as jnp
from jax import lax
from jax.sharding import PartitionSpec as P

D = 1024
P_SIZE = 64
N = 128
CONV = 4
BLOCK = 256
DI = 2048


EPSILON = 1e-05
PRECISE = lax.Precision.HIGH


def from_behind(shard, axis, by):
    devices = lax.axis_size(axis)
    pairs = [(i, i + by) for i in range(devices) if 0 <= i + by < devices]
    return lax.ppermute(shard, axis, pairs)


def chain_exchange(part, decays, axis, reverse):
    count = lax.axis_size(axis)
    rows = part.shape[0] * part.shape[1]
    share = rows // count
    got = lax.all_to_all(part.reshape(count, share, part.shape[2]), axis, 0, 0)
    row_decays = lax.dynamic_slice_in_dim(
        jnp.repeat(decays, part.shape[1], axis=1), lax.axis_index(axis) * share, share, 1
    )
    entering = [None] * count
    running = jnp.zeros_like(got[0])
    for place in reversed(range(count)) if reverse else range(count):
        entering[place] = running
        running = row_decays[place][:, None] * running + got[place]
    back = lax.all_to_all(jnp.stack(entering), axis, 0, 0)
    return back.reshape(part.shape)


def plain_dot(left, right):
    return jnp.dot(left, right, preferred_element_type=jnp.float32)


def contract_rows(left, right):
    return lax.dot_general(
        left, right, (((0,), (0,)), ((), ())), preferred_element_type=jnp.float32
    )


def contract_cols(left, right):
    return lax.dot_general(
        left, right, (((1,), (1,)), ((), ())), preferred_element_type=jnp.float32
    )


def silu_slope(value):
    sigma = jax.nn.sigmoid(value)
    return sigma * (1.0 + value * (1.0 - sigma))


def doc_number(doc_starts, positions):
    return jnp.sum((doc_starts[None, :] <= positions[:, None]).astype(jnp.int32), axis=1)


def block_terms(log_decay, doc_block, doc_before):
    cum_decay = jnp.cumsum(log_decay, axis=0)
    causal = jnp.arange(BLOCK)[:, None] >= jnp.arange(BLOCK)[None, :]
    same = (doc_block[:, None] == doc_block[None, :]) & causal
    spread = cum_decay.T[:, :, None] - cum_decay.T[:, None, :]
    decay = jnp.where(same[None], jnp.exp(jnp.minimum(spread, 0.0)), 0.0)
    carry_in = jnp.where((doc_block == doc_before)[:, None], jnp.exp(cum_decay), 0.0)
    to_end = jnp.where(
        (doc_block == doc_block[-1])[:, None], jnp.exp(cum_decay[-1][None, :] - cum_decay), 0.0
    )
    whole = jnp.where(doc_block[-1] == doc_before, jnp.exp(cum_decay[-1]), 0.0)
    return (decay, carry_in, to_end, whole)


def block_forward_local(scaled, in_mat, out_mat, log_decay, doc_block, doc_before):
    decay, carry_in, to_end, whole = block_terms(log_decay, doc_block, doc_before)
    scores = jnp.dot(out_mat, in_mat.T, precision=PRECISE)
    y_inner = jnp.einsum("hij,ij,jhp->ihp", decay, scores, scaled, precision=PRECISE)
    block_state = jnp.einsum("jh,jhp,jn->hpn", to_end, scaled, in_mat, precision=PRECISE)
    return (y_inner, block_state, whole, carry_in)


def block_local_grad(grad_y, scaled, in_mat, out_mat, log_decay, doc_block, doc_before, state):
    decay, carry_in, to_end, whole = block_terms(log_decay, doc_block, doc_before)
    scores = jnp.dot(out_mat, in_mat.T, precision=PRECISE)
    inner = jnp.einsum("ihp,jhp->hij", grad_y, scaled, precision=PRECISE)
    grad_scores = jnp.sum(inner * decay, axis=0)
    grad_decay = inner * scores[None] * decay
    grad_cum = jnp.sum(grad_decay, axis=2).T - jnp.sum(grad_decay, axis=1).T
    grad_scaled = jnp.einsum("hij,ij,ihp->jhp", decay, scores, grad_y, precision=PRECISE)
    grad_out = jnp.dot(grad_scores, in_mat, precision=PRECISE)
    grad_in = jnp.dot(grad_scores.T, out_mat, precision=PRECISE)
    readout = jnp.einsum("in,hpn->ihp", out_mat, state, precision=PRECISE)
    grad_cum = grad_cum + jnp.sum(grad_y * readout, axis=2) * carry_in
    grad_out = grad_out + jnp.einsum("ih,ihp,hpn->in", carry_in, grad_y, state, precision=PRECISE)
    local_grad = jnp.einsum("ih,ihp,in->hpn", carry_in, grad_y, out_mat, precision=PRECISE)
    return (grad_scaled, grad_in, grad_out, grad_cum, local_grad, to_end)


def block_state_grad(grad_after, scaled, in_mat, to_end, whole, state, grad_cum):
    grad_end = jnp.einsum("hpn,jhp,jn->jh", grad_after, scaled, in_mat, precision=PRECISE)
    more_scaled = jnp.einsum("jh,jn,hpn->jhp", to_end, in_mat, grad_after, precision=PRECISE)
    more_in = jnp.einsum("jh,jhp,hpn->jn", to_end, scaled, grad_after, precision=PRECISE)
    weighted = grad_end * to_end
    grad_whole = jnp.sum(grad_after * state, axis=(1, 2))
    grad_cum = grad_cum - weighted
    grad_cum = grad_cum.at[-1].add(jnp.sum(weighted, axis=0) + grad_whole * whole)
    grad_log = jnp.cumsum(grad_cum[::-1], axis=0)[::-1]
    return (more_scaled, more_in, grad_log)


def shards(
    hidden_in,
    norm_gain,
    proj_gate,
    proj_value,
    proj_inout,
    proj_step,
    conv_value,
    conv_bias_value,
    conv_inout,
    conv_bias_inout,
    step_bias,
    decay_log,
    skip_gain,
    gate_gain,
    proj_out,
    out_grad,
    doc_starts,
):
    tokens_dev = hidden_in.shape[0]
    heads_here = proj_step.shape[1]
    inner = proj_gate.shape[1]
    head_count = lax.axis_size("head")
    head_rank = lax.axis_index("head")
    seq_rank = lax.axis_index("seq")
    inout_cols = 2 * N // head_count
    col_start = head_rank * inout_cols
    feat_cols = D // head_count
    feat_start = head_rank * feat_cols
    blocks = tokens_dev // BLOCK
    margin = CONV - 1
    rows_full, grad_full = (
        lax.all_gather(hidden_in, "head", axis=1, tiled=True),
        lax.all_gather(out_grad, "head", axis=1, tiled=True),
    )
    x_float = rows_full.astype(jnp.float32)
    inv_rms = lax.rsqrt(jnp.mean(x_float * x_float, axis=1) + EPSILON)
    normed = (x_float * inv_rms[:, None] * norm_gain[None, :]).astype(jnp.bfloat16)
    gate_pre = plain_dot(normed, proj_gate)
    conv_in = jnp.concatenate(
        [plain_dot(normed, proj_value), plain_dot(normed, proj_inout)], axis=1
    ).astype(jnp.bfloat16)
    step_raw = plain_dot(normed, proj_step)
    tail_prev = from_behind(conv_in[tokens_dev - margin :], "seq", 1)
    first_pos = seq_rank * tokens_dev
    doc_ids = doc_number(doc_starts, first_pos + jnp.arange(tokens_dev, dtype=jnp.int32))
    doc_margin = doc_number(doc_starts, first_pos - margin + jnp.arange(margin, dtype=jnp.int32))
    doc_before = doc_number(doc_starts, first_pos - 1 + BLOCK * jnp.arange(blocks, dtype=jnp.int32))
    conv_pad = jnp.concatenate([tail_prev, conv_in], axis=0).astype(jnp.float32)
    doc_pad = jnp.concatenate([doc_margin, doc_ids])
    conv_weight = jnp.concatenate([conv_value, conv_inout], axis=1)
    conv_bias = jnp.concatenate([conv_bias_value, conv_bias_inout])
    lag_masks = [
        (doc_pad[margin - offset : margin - offset + tokens_dev] == doc_ids).astype(jnp.float32)[
            :, None
        ]
        for offset in range(CONV)
    ]
    conv_pre = conv_bias[None, :] + sum(
        (
            conv_weight[offset][None, :]
            * conv_pad[margin - offset : margin - offset + tokens_dev]
            * lag_masks[offset]
            for offset in range(CONV)
        )
    )
    conv_act = jax.nn.silu(conv_pre)
    values = conv_act[:, :inner].reshape(tokens_dev, heads_here, P_SIZE)
    in_mat = conv_act[:, inner : inner + N]
    out_mat = conv_act[:, inner + N :]
    step_size = jax.nn.softplus(step_raw + step_bias[None, :])
    decay_rate = -jnp.exp(decay_log)
    log_decay = step_size * decay_rate[None, :]
    scaled = values * step_size[:, :, None]

    def by_block(array):
        return array.reshape((blocks, BLOCK) + array.shape[1:])

    blk_scaled = by_block(scaled)
    blk_in = by_block(in_mat)
    blk_out = by_block(out_mat)
    blk_log = by_block(log_decay)
    blk_docs = by_block(doc_ids)
    y_inner, block_states, wholes, carries = jax.vmap(block_forward_local)(
        blk_scaled, blk_in, blk_out, blk_log, blk_docs, doc_before
    )
    dev_decay = jnp.ones((heads_here,), jnp.float32)
    dev_state = jnp.zeros((heads_here, P_SIZE, N), jnp.float32)
    for block in range(blocks):
        dev_decay = wholes[block] * dev_decay
        dev_state = wholes[block][:, None, None] * dev_state + block_states[block]
    decays_all = lax.all_gather(dev_decay, "seq")
    state_in = chain_exchange(dev_state, decays_all, "seq", False)
    entering_list = []
    running = state_in
    for block in range(blocks):
        entering_list.append(running)
        running = wholes[block][:, None, None] * running + block_states[block]
    entering = jnp.stack(entering_list)
    y_state = carries[..., None] * jnp.einsum(
        "cin,chpn->cihp", blk_out, entering, precision=PRECISE
    )
    y_ssd = (y_inner + y_state).reshape(tokens_dev, heads_here, P_SIZE) + skip_gain[
        None, :, None
    ] * values
    y_flat = y_ssd.reshape(tokens_dev, inner)
    gate_act = jax.nn.silu(gate_pre)
    gated = y_flat * gate_act
    grad_normed_gate = contract_cols(grad_full, proj_out)
    gate_term = grad_normed_gate * gate_gain[None, :]
    gate_sq, gate_dot = lax.psum(
        jnp.stack([jnp.sum(gated * gated, axis=1), jnp.sum(gate_term * gated, axis=1)]), "head"
    )
    inv_gate = lax.rsqrt(gate_sq / DI + EPSILON)
    normed_gate = (gated * inv_gate[:, None] * gate_gain[None, :]).astype(jnp.bfloat16)
    proj_part = lax.psum_scatter(
        contract_rows(proj_out, normed_gate.T), "head", scatter_dimension=0, tiled=True
    )
    x_own = hidden_in.astype(jnp.float32)
    block_out = (x_own + proj_part.T).astype(jnp.bfloat16)
    grad_w_out = contract_rows(grad_full, normed_gate)
    grad_gate_gain = jnp.sum(grad_normed_gate * gated * inv_gate[:, None], axis=0)
    grad_gated = inv_gate[:, None] * gate_term - gated * (inv_gate**3 * gate_dot / DI)[:, None]
    grad_y = (grad_gated * gate_act).reshape(tokens_dev, heads_here, P_SIZE)
    grad_gate_pre = grad_gated * y_flat * silu_slope(gate_pre)
    grad_skip = jnp.sum(grad_y * values, axis=(0, 2))
    part_scaled, part_in, part_out, part_cum, local_grads, to_ends = jax.vmap(block_local_grad)(
        by_block(grad_y), blk_scaled, blk_in, blk_out, blk_log, blk_docs, doc_before, entering
    )
    dev_grad = jnp.zeros((heads_here, P_SIZE, N), jnp.float32)
    prefix = jnp.ones((heads_here,), jnp.float32)
    for block in range(blocks):
        dev_grad = dev_grad + prefix[:, None, None] * local_grads[block]
        prefix = prefix * wholes[block]
    grad_out_state = chain_exchange(dev_grad, decays_all, "seq", True)
    after_list = [None] * blocks
    running = grad_out_state
    for block in reversed(range(blocks)):
        after_list[block] = running
        running = wholes[block][:, None, None] * running + local_grads[block]
    grad_after = jnp.stack(after_list)
    more_scaled, more_in, grad_log = jax.vmap(block_state_grad)(
        grad_after, blk_scaled, blk_in, to_ends, wholes, entering, part_cum
    )
    grad_scaled = (part_scaled + more_scaled).reshape(tokens_dev, heads_here, P_SIZE)
    grad_in_mat = (part_in + more_in).reshape(tokens_dev, N)
    grad_out_mat = part_out.reshape(tokens_dev, N)
    grad_log = grad_log.reshape(tokens_dev, heads_here)
    grad_values = grad_scaled * step_size[:, :, None] + skip_gain[None, :, None] * grad_y
    grad_step = grad_log * decay_rate[None, :] + jnp.sum(grad_scaled * values, axis=2)
    grad_decay_log = jnp.sum(grad_log * step_size, axis=0) * decay_rate
    grad_step_raw = grad_step * jax.nn.sigmoid(step_raw + step_bias[None, :])
    grad_step_bias = jnp.sum(grad_step_raw, axis=0)
    inout_sum = lax.psum_scatter(
        jnp.concatenate([grad_in_mat, grad_out_mat], axis=1),
        "head",
        scatter_dimension=1,
        tiled=True,
    )
    pre_sel = jnp.concatenate(
        [
            conv_pre[:, :inner],
            lax.dynamic_slice_in_dim(conv_pre[:, inner:], col_start, inout_cols, 1),
        ],
        axis=1,
    )
    pad_sel = jnp.concatenate(
        [
            conv_pad[:, :inner],
            lax.dynamic_slice_in_dim(conv_pad[:, inner:], col_start, inout_cols, 1),
        ],
        axis=1,
    )
    weight_sel = jnp.concatenate(
        [conv_value, lax.dynamic_slice_in_dim(conv_inout, col_start, inout_cols, 1)], axis=1
    )
    grad_act = jnp.concatenate([grad_values.reshape(tokens_dev, inner), inout_sum], axis=1)
    grad_pre = grad_act * silu_slope(pre_sel)
    grad_conv = jnp.stack(
        [
            jnp.sum(
                grad_pre
                * pad_sel[margin - offset : margin - offset + tokens_dev]
                * lag_masks[offset],
                axis=0,
            )
            for offset in range(CONV)
        ]
    )
    grad_conv_bias = jnp.sum(grad_pre, axis=0)
    grad_pad = sum(
        (
            jnp.pad(
                grad_pre * weight_sel[offset][None, :] * lag_masks[offset],
                ((margin - offset, offset), (0, 0)),
            )
            for offset in range(CONV)
        )
    )
    tail_grad = from_behind(grad_pad[:margin], "seq", -1)
    grad_conv_in = grad_pad[margin:] + jnp.pad(tail_grad, ((tokens_dev - margin, 0), (0, 0)))
    grad_gate_b = grad_gate_pre.astype(jnp.bfloat16)
    grad_value_b = grad_conv_in[:, :inner].astype(jnp.bfloat16)
    grad_inout_b = grad_conv_in[:, inner:].astype(jnp.bfloat16)
    grad_step_b = grad_step_raw.astype(jnp.bfloat16)
    inout_weight = lax.dynamic_slice_in_dim(proj_inout, col_start, inout_cols, 1)
    pieces = (
        (grad_gate_b, proj_gate),
        (grad_value_b, proj_value),
        (grad_inout_b, inout_weight),
        (grad_step_b, proj_step),
    )
    own_gain = lax.dynamic_slice_in_dim(norm_gain, feat_start, feat_cols, 0)
    full_term = sum((contract_cols(grad_part, weight) for grad_part, weight in pieces))
    row_part = jnp.sum(full_term * norm_gain[None, :] * x_float, axis=1)
    gain_part = jnp.sum(full_term * x_float * inv_rms[:, None], axis=0)
    head_sums = lax.psum(jnp.concatenate([row_part, gain_part]), "head")
    row_dot = head_sums[:tokens_dev] / D
    grad_norm_part = lax.dynamic_slice_in_dim(head_sums, tokens_dev + feat_start, feat_cols, 0)
    shares = jnp.moveaxis(full_term.reshape(tokens_dev, head_count, feat_cols), 1, 0)
    shares = lax.all_to_all(shares.astype(jnp.bfloat16), "head", 0, 0)
    grad_normed = jnp.sum(shares.astype(jnp.float32), axis=0)
    norm_term = grad_normed * own_gain[None, :]
    grad_in = (
        out_grad.astype(jnp.float32)
        + inv_rms[:, None] * norm_term
        - x_own * (inv_rms**3 * row_dot)[:, None]
    )
    seq_count = lax.axis_size("seq")
    grad_pre_b = jnp.concatenate([piece for piece, _ in pieces], axis=1)
    weight_grads = jnp.concatenate([contract_rows(normed, grad_pre_b), grad_w_out], axis=1)
    weight_grads = weight_grads.astype(jnp.bfloat16).reshape(seq_count, D // seq_count, -1)
    weight_grads = lax.all_to_all(weight_grads, "seq", 0, 0)
    weight_grads = jnp.sum(weight_grads.astype(jnp.float32), axis=0)
    ends = [inner, 2 * inner, 2 * inner + inout_cols, 2 * inner + inout_cols + heads_here]
    big_grads = jnp.split(weight_grads, ends, axis=1)
    small_parts = (
        grad_conv,
        grad_conv_bias,
        grad_step_bias,
        grad_decay_log,
        grad_skip,
        grad_gate_gain,
        grad_norm_part,
    )
    flat = lax.psum(jnp.concatenate([part.reshape(-1) for part in small_parts]), "seq")
    small = []
    start = 0
    for part in small_parts:
        small.append(flat[start : start + part.size].reshape(part.shape))
        start += part.size
    conv_total = small[0]
    conv_bias_total = small[1]
    return (
        block_out,
        grad_in,
        small[6],
        big_grads[0],
        big_grads[1],
        big_grads[2],
        big_grads[3],
        conv_total[:, :inner],
        conv_bias_total[:inner],
        conv_total[:, inner:],
        conv_bias_total[inner:],
        small[2],
        small[3],
        small[4],
        small[5],
        big_grads[4].T,
    )


def solution(mesh):
    in_specs = (
        P("seq", "head"),
        P(),
        P(None, "head"),
        P(None, "head"),
        P(),
        P(None, "head"),
        P(None, "head"),
        P("head"),
        P(),
        P(),
        P("head"),
        P("head"),
        P("head"),
        P("head"),
        P("head", None),
        P("seq", "head"),
        P(),
    )
    out_specs = (
        P("seq", "head"),
        P("seq", "head"),
        P("head"),
        P("seq", "head"),
        P("seq", "head"),
        P("seq", "head"),
        P("seq", "head"),
        P(None, "head"),
        P("head"),
        P(None, "head"),
        P("head"),
        P("head"),
        P("head"),
        P("head"),
        P("head"),
        P("head", "seq"),
    )
    return jax.shard_map(shards, mesh=mesh, in_specs=in_specs, out_specs=out_specs, check_vma=False)
```

```python
import jax
import jax.numpy as jnp
from jax import lax
from jax.sharding import PartitionSpec as P

D = 1024
P_SIZE = 64
N = 128
CONV = 4
BLOCK = 256
DI = 2048


EPSILON = 1e-05
PRECISE = lax.Precision.HIGH


def from_behind(shard, axis, by):
    devices = lax.axis_size(axis)
    pairs = [(i, i + by) for i in range(devices) if 0 <= i + by < devices]
    return lax.ppermute(shard, axis, pairs)


def chain_exchange(part, decays, axis, reverse):
    count = lax.axis_size(axis)
    rows = part.shape[0] * part.shape[1]
    share = rows // count
    got = lax.all_to_all(part.reshape(count, share, part.shape[2]), axis, 0, 0)
    row_decays = lax.dynamic_slice_in_dim(
        jnp.repeat(decays, part.shape[1], axis=1), lax.axis_index(axis) * share, share, 1
    )
    entering = [None] * count
    running = jnp.zeros_like(got[0])
    for place in reversed(range(count)) if reverse else range(count):
        entering[place] = running
        running = row_decays[place][:, None] * running + got[place]
    back = lax.all_to_all(jnp.stack(entering), axis, 0, 0)
    return back.reshape(part.shape)


def plain_dot(left, right):
    return jnp.dot(left, right, preferred_element_type=jnp.float32)


def contract_rows(left, right):
    return lax.dot_general(
        left, right, (((0,), (0,)), ((), ())), preferred_element_type=jnp.float32
    )


def contract_cols(left, right):
    return lax.dot_general(
        left, right, (((1,), (1,)), ((), ())), preferred_element_type=jnp.float32
    )


def silu_slope(value):
    sigma = jax.nn.sigmoid(value)
    return sigma * (1.0 + value * (1.0 - sigma))


def doc_number(doc_starts, positions):
    return jnp.sum((doc_starts[None, :] <= positions[:, None]).astype(jnp.int32), axis=1)


def block_terms(log_decay, doc_block, doc_before):
    cum_decay = jnp.cumsum(log_decay, axis=0)
    causal = jnp.arange(BLOCK)[:, None] >= jnp.arange(BLOCK)[None, :]
    same = (doc_block[:, None] == doc_block[None, :]) & causal
    spread = cum_decay.T[:, :, None] - cum_decay.T[:, None, :]
    decay = jnp.where(same[None], jnp.exp(jnp.minimum(spread, 0.0)), 0.0)
    carry_in = jnp.where((doc_block == doc_before)[:, None], jnp.exp(cum_decay), 0.0)
    to_end = jnp.where(
        (doc_block == doc_block[-1])[:, None], jnp.exp(cum_decay[-1][None, :] - cum_decay), 0.0
    )
    whole = jnp.where(doc_block[-1] == doc_before, jnp.exp(cum_decay[-1]), 0.0)
    return (decay, carry_in, to_end, whole)


def block_forward_local(scaled, in_mat, out_mat, log_decay, doc_block, doc_before):
    decay, carry_in, to_end, whole = block_terms(log_decay, doc_block, doc_before)
    scores = jnp.dot(out_mat, in_mat.T, precision=PRECISE)
    y_inner = jnp.einsum("hij,ij,jhp->ihp", decay, scores, scaled, precision=PRECISE)
    block_state = jnp.einsum("jh,jhp,jn->hpn", to_end, scaled, in_mat, precision=PRECISE)
    return (y_inner, block_state, whole, carry_in)


def block_local_grad(grad_y, scaled, in_mat, out_mat, log_decay, doc_block, doc_before, state):
    decay, carry_in, to_end, whole = block_terms(log_decay, doc_block, doc_before)
    scores = jnp.dot(out_mat, in_mat.T, precision=PRECISE)
    inner = jnp.einsum("ihp,jhp->hij", grad_y, scaled, precision=PRECISE)
    grad_scores = jnp.sum(inner * decay, axis=0)
    grad_decay = inner * scores[None] * decay
    grad_cum = jnp.sum(grad_decay, axis=2).T - jnp.sum(grad_decay, axis=1).T
    grad_scaled = jnp.einsum("hij,ij,ihp->jhp", decay, scores, grad_y, precision=PRECISE)
    grad_out = jnp.dot(grad_scores, in_mat, precision=PRECISE)
    grad_in = jnp.dot(grad_scores.T, out_mat, precision=PRECISE)
    readout = jnp.einsum("in,hpn->ihp", out_mat, state, precision=PRECISE)
    grad_cum = grad_cum + jnp.sum(grad_y * readout, axis=2) * carry_in
    grad_out = grad_out + jnp.einsum("ih,ihp,hpn->in", carry_in, grad_y, state, precision=PRECISE)
    local_grad = jnp.einsum("ih,ihp,in->hpn", carry_in, grad_y, out_mat, precision=PRECISE)
    return (grad_scaled, grad_in, grad_out, grad_cum, local_grad, to_end)


def block_state_grad(grad_after, scaled, in_mat, to_end, whole, state, grad_cum):
    grad_end = jnp.einsum("hpn,jhp,jn->jh", grad_after, scaled, in_mat, precision=PRECISE)
    more_scaled = jnp.einsum("jh,jn,hpn->jhp", to_end, in_mat, grad_after, precision=PRECISE)
    more_in = jnp.einsum("jh,jhp,hpn->jn", to_end, scaled, grad_after, precision=PRECISE)
    weighted = grad_end * to_end
    grad_whole = jnp.sum(grad_after * state, axis=(1, 2))
    grad_cum = grad_cum - weighted
    grad_cum = grad_cum.at[-1].add(jnp.sum(weighted, axis=0) + grad_whole * whole)
    grad_log = jnp.cumsum(grad_cum[::-1], axis=0)[::-1]
    return (more_scaled, more_in, grad_log)


def shards(
    hidden_in,
    norm_gain,
    proj_gate,
    proj_value,
    proj_inout,
    proj_step,
    conv_value,
    conv_bias_value,
    conv_inout,
    conv_bias_inout,
    step_bias,
    decay_log,
    skip_gain,
    gate_gain,
    proj_out,
    out_grad,
    doc_starts,
):
    tokens_dev = hidden_in.shape[0]
    heads_here = proj_step.shape[1]
    inner = proj_gate.shape[1]
    head_count = lax.axis_size("head")
    head_rank = lax.axis_index("head")
    seq_rank = lax.axis_index("seq")
    inout_cols = 2 * N // head_count
    col_start = head_rank * inout_cols
    feat_cols = D // head_count
    feat_start = head_rank * feat_cols
    blocks = tokens_dev // BLOCK
    margin = CONV - 1
    rows_full, grad_full = (
        lax.all_gather(hidden_in, "head", axis=1, tiled=True),
        lax.all_gather(out_grad, "head", axis=1, tiled=True),
    )
    x_float = rows_full.astype(jnp.float32)
    inv_rms = lax.rsqrt(jnp.mean(x_float * x_float, axis=1) + EPSILON)
    normed = (x_float * inv_rms[:, None] * norm_gain[None, :]).astype(jnp.bfloat16)
    gate_pre = plain_dot(normed, proj_gate)
    conv_in = jnp.concatenate(
        [plain_dot(normed, proj_value), plain_dot(normed, proj_inout)], axis=1
    ).astype(jnp.bfloat16)
    step_raw = plain_dot(normed, proj_step)
    tail_prev = from_behind(conv_in[tokens_dev - margin :], "seq", 1)
    first_pos = seq_rank * tokens_dev
    doc_ids = doc_number(doc_starts, first_pos + jnp.arange(tokens_dev, dtype=jnp.int32))
    doc_margin = doc_number(doc_starts, first_pos - margin + jnp.arange(margin, dtype=jnp.int32))
    doc_before = doc_number(doc_starts, first_pos - 1 + BLOCK * jnp.arange(blocks, dtype=jnp.int32))
    conv_pad = jnp.concatenate([tail_prev, conv_in], axis=0).astype(jnp.float32)
    doc_pad = jnp.concatenate([doc_margin, doc_ids])
    conv_weight = jnp.concatenate([conv_value, conv_inout], axis=1)
    conv_bias = jnp.concatenate([conv_bias_value, conv_bias_inout])
    lag_masks = [
        (doc_pad[margin - offset : margin - offset + tokens_dev] == doc_ids).astype(jnp.float32)[
            :, None
        ]
        for offset in range(CONV)
    ]
    conv_pre = conv_bias[None, :] + sum(
        (
            conv_weight[offset][None, :]
            * conv_pad[margin - offset : margin - offset + tokens_dev]
            * lag_masks[offset]
            for offset in range(CONV)
        )
    )
    conv_act = jax.nn.silu(conv_pre)
    values = conv_act[:, :inner].reshape(tokens_dev, heads_here, P_SIZE)
    in_mat = conv_act[:, inner : inner + N]
    out_mat = conv_act[:, inner + N :]
    step_size = jax.nn.softplus(step_raw + step_bias[None, :])
    decay_rate = -jnp.exp(decay_log)
    log_decay = step_size * decay_rate[None, :]
    scaled = values * step_size[:, :, None]

    def by_block(array):
        return array.reshape((blocks, BLOCK) + array.shape[1:])

    blk_scaled = by_block(scaled)
    blk_in = by_block(in_mat)
    blk_out = by_block(out_mat)
    blk_log = by_block(log_decay)
    blk_docs = by_block(doc_ids)
    y_inner, block_states, wholes, carries = jax.vmap(block_forward_local)(
        blk_scaled, blk_in, blk_out, blk_log, blk_docs, doc_before
    )
    dev_decay = jnp.ones((heads_here,), jnp.float32)
    dev_state = jnp.zeros((heads_here, P_SIZE, N), jnp.float32)
    for block in range(blocks):
        dev_decay = wholes[block] * dev_decay
        dev_state = wholes[block][:, None, None] * dev_state + block_states[block]
    seq_count = lax.axis_size("seq")
    decays_all = lax.all_to_all(
        jnp.broadcast_to(dev_decay[None], (seq_count, heads_here)), "seq", 0, 0
    )
    state_in = chain_exchange(dev_state, decays_all, "seq", False)
    entering_list = []
    running = state_in
    for block in range(blocks):
        entering_list.append(running)
        running = wholes[block][:, None, None] * running + block_states[block]
    entering = jnp.stack(entering_list)
    y_state = carries[..., None] * jnp.einsum(
        "cin,chpn->cihp", blk_out, entering, precision=PRECISE
    )
    y_ssd = (y_inner + y_state).reshape(tokens_dev, heads_here, P_SIZE) + skip_gain[
        None, :, None
    ] * values
    y_flat = y_ssd.reshape(tokens_dev, inner)
    gate_act = jax.nn.silu(gate_pre)
    gated = y_flat * gate_act
    grad_normed_gate = contract_cols(grad_full, proj_out)
    gate_term = grad_normed_gate * gate_gain[None, :]
    gate_sq, gate_dot = lax.psum(
        jnp.stack([jnp.sum(gated * gated, axis=1), jnp.sum(gate_term * gated, axis=1)]), "head"
    )
    inv_gate = lax.rsqrt(gate_sq / DI + EPSILON)
    normed_gate = (gated * inv_gate[:, None] * gate_gain[None, :]).astype(jnp.bfloat16)
    proj_part = lax.psum_scatter(
        contract_rows(proj_out, normed_gate.T), "head", scatter_dimension=0, tiled=True
    )
    x_own = hidden_in.astype(jnp.float32)
    block_out = (x_own + proj_part.T).astype(jnp.bfloat16)
    grad_w_out = contract_rows(grad_full, normed_gate)
    grad_gate_gain = jnp.sum(grad_normed_gate * gated * inv_gate[:, None], axis=0)
    grad_gated = inv_gate[:, None] * gate_term - gated * (inv_gate**3 * gate_dot / DI)[:, None]
    grad_y = (grad_gated * gate_act).reshape(tokens_dev, heads_here, P_SIZE)
    grad_gate_pre = grad_gated * y_flat * silu_slope(gate_pre)
    grad_skip = jnp.sum(grad_y * values, axis=(0, 2))
    part_scaled, part_in, part_out, part_cum, local_grads, to_ends = jax.vmap(block_local_grad)(
        by_block(grad_y), blk_scaled, blk_in, blk_out, blk_log, blk_docs, doc_before, entering
    )
    dev_grad = jnp.zeros((heads_here, P_SIZE, N), jnp.float32)
    prefix = jnp.ones((heads_here,), jnp.float32)
    for block in range(blocks):
        dev_grad = dev_grad + prefix[:, None, None] * local_grads[block]
        prefix = prefix * wholes[block]
    grad_out_state = chain_exchange(dev_grad, decays_all, "seq", True)
    grad_gate_b = grad_gate_pre.astype(jnp.bfloat16)
    early = jnp.concatenate([contract_rows(normed, grad_gate_b), grad_w_out], axis=1)
    early = early.astype(jnp.bfloat16).reshape(seq_count, D // seq_count, -1)
    early, grad_out_state = lax.optimization_barrier((early, grad_out_state))
    early = lax.all_to_all(early, "seq", 0, 0)
    after_list = [None] * blocks
    running = grad_out_state
    for block in reversed(range(blocks)):
        after_list[block] = running
        running = wholes[block][:, None, None] * running + local_grads[block]
    grad_after = jnp.stack(after_list)
    more_scaled, more_in, grad_log = jax.vmap(block_state_grad)(
        grad_after, blk_scaled, blk_in, to_ends, wholes, entering, part_cum
    )
    grad_scaled = (part_scaled + more_scaled).reshape(tokens_dev, heads_here, P_SIZE)
    grad_in_mat = (part_in + more_in).reshape(tokens_dev, N)
    grad_out_mat = part_out.reshape(tokens_dev, N)
    grad_log = grad_log.reshape(tokens_dev, heads_here)
    grad_values = grad_scaled * step_size[:, :, None] + skip_gain[None, :, None] * grad_y
    grad_step = grad_log * decay_rate[None, :] + jnp.sum(grad_scaled * values, axis=2)
    grad_decay_log = jnp.sum(grad_log * step_size, axis=0) * decay_rate
    grad_step_raw = grad_step * jax.nn.sigmoid(step_raw + step_bias[None, :])
    grad_step_bias = jnp.sum(grad_step_raw, axis=0)
    inout_sum = lax.psum_scatter(
        jnp.concatenate([grad_in_mat, grad_out_mat], axis=1),
        "head",
        scatter_dimension=1,
        tiled=True,
    )
    early, inout_sum = lax.optimization_barrier((early, inout_sum))
    pre_sel = jnp.concatenate(
        [
            conv_pre[:, :inner],
            lax.dynamic_slice_in_dim(conv_pre[:, inner:], col_start, inout_cols, 1),
        ],
        axis=1,
    )
    pad_sel = jnp.concatenate(
        [
            conv_pad[:, :inner],
            lax.dynamic_slice_in_dim(conv_pad[:, inner:], col_start, inout_cols, 1),
        ],
        axis=1,
    )
    weight_sel = jnp.concatenate(
        [conv_value, lax.dynamic_slice_in_dim(conv_inout, col_start, inout_cols, 1)], axis=1
    )
    grad_act = jnp.concatenate([grad_values.reshape(tokens_dev, inner), inout_sum], axis=1)
    grad_pre = grad_act * silu_slope(pre_sel)
    grad_conv = jnp.stack(
        [
            jnp.sum(
                grad_pre
                * pad_sel[margin - offset : margin - offset + tokens_dev]
                * lag_masks[offset],
                axis=0,
            )
            for offset in range(CONV)
        ]
    )
    grad_conv_bias = jnp.sum(grad_pre, axis=0)
    grad_pad = sum(
        (
            jnp.pad(
                grad_pre * weight_sel[offset][None, :] * lag_masks[offset],
                ((margin - offset, offset), (0, 0)),
            )
            for offset in range(CONV)
        )
    )
    tail_grad = from_behind(grad_pad[:margin], "seq", -1)
    grad_conv_in = grad_pad[margin:] + jnp.pad(tail_grad, ((tokens_dev - margin, 0), (0, 0)))
    grad_value_b = grad_conv_in[:, :inner].astype(jnp.bfloat16)
    grad_inout_b = grad_conv_in[:, inner:].astype(jnp.bfloat16)
    grad_step_b = grad_step_raw.astype(jnp.bfloat16)
    inout_weight = lax.dynamic_slice_in_dim(proj_inout, col_start, inout_cols, 1)
    pieces = (
        (grad_gate_b, proj_gate),
        (grad_value_b, proj_value),
        (grad_inout_b, inout_weight),
        (grad_step_b, proj_step),
    )
    own_gain = lax.dynamic_slice_in_dim(norm_gain, feat_start, feat_cols, 0)
    full_term = sum((contract_cols(grad_part, weight) for grad_part, weight in pieces))
    row_part = jnp.sum(full_term * norm_gain[None, :] * x_float, axis=1)
    gain_part = jnp.sum(full_term * x_float * inv_rms[:, None], axis=0)
    head_sums = lax.psum(jnp.concatenate([row_part, gain_part]), "head")
    row_dot = head_sums[:tokens_dev] / D
    grad_norm_part = lax.dynamic_slice_in_dim(head_sums, tokens_dev + feat_start, feat_cols, 0)
    shares = jnp.moveaxis(full_term.reshape(tokens_dev, head_count, feat_cols), 1, 0)
    shares = lax.all_to_all(shares.astype(jnp.bfloat16), "head", 0, 0)
    grad_normed = jnp.sum(shares.astype(jnp.float32), axis=0)
    norm_term = grad_normed * own_gain[None, :]
    grad_in = (
        out_grad.astype(jnp.float32)
        + inv_rms[:, None] * norm_term
        - x_own * (inv_rms**3 * row_dot)[:, None]
    )
    grad_pre_b = jnp.concatenate([piece for piece, _ in pieces[1:]], axis=1)
    weight_grads = contract_rows(normed, grad_pre_b)
    weight_grads = weight_grads.astype(jnp.bfloat16).reshape(seq_count, D // seq_count, -1)
    weight_grads = lax.all_to_all(weight_grads, "seq", 0, 0)
    weight_grads = jnp.sum(weight_grads.astype(jnp.float32), axis=0)
    value_grad, inout_grad, step_grad = jnp.split(weight_grads, [inner, inner + inout_cols], axis=1)
    early = jnp.sum(early.astype(jnp.float32), axis=0)
    big_grads = (early[:, :inner], value_grad, inout_grad, step_grad, early[:, inner:])
    small_parts = (
        grad_conv,
        grad_conv_bias,
        grad_step_bias,
        grad_decay_log,
        grad_skip,
        grad_gate_gain,
        grad_norm_part,
    )
    flat = lax.psum(jnp.concatenate([part.reshape(-1) for part in small_parts]), "seq")
    small = []
    start = 0
    for part in small_parts:
        small.append(flat[start : start + part.size].reshape(part.shape))
        start += part.size
    conv_total = small[0]
    conv_bias_total = small[1]
    return (
        block_out,
        grad_in,
        small[6],
        big_grads[0],
        big_grads[1],
        big_grads[2],
        big_grads[3],
        conv_total[:, :inner],
        conv_bias_total[:inner],
        conv_total[:, inner:],
        conv_bias_total[inner:],
        small[2],
        small[3],
        small[4],
        small[5],
        big_grads[4].T,
    )


def solution(mesh):
    in_specs = (
        P("seq", "head"),
        P(),
        P(None, "head"),
        P(None, "head"),
        P(),
        P(None, "head"),
        P(None, "head"),
        P("head"),
        P(),
        P(),
        P("head"),
        P("head"),
        P("head"),
        P("head"),
        P("head", None),
        P("seq", "head"),
        P(),
    )
    out_specs = (
        P("seq", "head"),
        P("seq", "head"),
        P("head"),
        P("seq", "head"),
        P("seq", "head"),
        P("seq", "head"),
        P("seq", "head"),
        P(None, "head"),
        P("head"),
        P(None, "head"),
        P("head"),
        P("head"),
        P("head"),
        P("head"),
        P("head"),
        P("head", "seq"),
    )
    return jax.shard_map(shards, mesh=mesh, in_specs=in_specs, out_specs=out_specs, check_vma=False)
```
